512 devices in a mesh: lat: 16 (over z_lo, core), lon: 32 (over x, y, z_hi).
Axes of the slice: x: 4, y: 4, z: 16 (z_hi: 2, z_lo: 8; z = z_hi * 8 + z_lo), core: 2. Of those that a mesh axis runs over, the one named last changes fastest.
Arguments:
- queries: bfloat16 [128, 512, 512], P('lat', 'lon'), may hold values from -180 to 180
- key_cells: bfloat16 [128, 512, 512], P('lat', 'lon'), may hold values from -15 to 15
- value_cells: bfloat16 [128, 512, 512], P('lat', 'lon'), may hold values from -5 to 5
- grad_output: bfloat16 [128, 512, 512], P('lat', 'lon'), may hold values from -5 to 5
- rel_bias: float32 [8, 169], replicated, may hold values from -4 to 4
Outputs:
- output: bfloat16 [128, 512, 512], P('lat', 'lon')
- grad_query: bfloat16 [128, 512, 512], P('lat', 'lon')
- grad_key: bfloat16 [128, 512, 512], P('lat', 'lon')
- grad_value: bfloat16 [128, 512, 512], P('lat', 'lon')
The draws below stay inside these ranges and needn't reach their ends.
All inputs are finite; a program needn't handle non-finite values.
Results may differ from the reference program's by a relative error of at most 0.009.
Values may be sent and summed in bfloat16 or wider, within the bound.
A program may use at most 64 MiB of HBM per device.

```python
import jax
import jax.numpy as jnp
from jax import lax

HEADS = 8
HEAD_DIM = 64
TILE = 8
RADIUS = 6
FEAT = 512
SPAN = 13
NLAT = 128
NLON = 512


def pair_fields(key):
    shape_all = (NLAT, NLON, HEADS * HEAD_DIM)
    query_draw = jnp.clip(jax.random.normal(jax.random.fold_in(key, 101), shape_all, jnp.float32), -5.0, 5.0)
    key_draw = jnp.clip(jax.random.normal(jax.random.fold_in(key, 102), shape_all, jnp.float32), -5.0, 5.0)
    return (query_draw, key_draw)


def draw_queries(key, part):
    return pair_fields(key)[0].astype(jnp.bfloat16)


def draw_key_cells(key, part):
    return pair_fields(key)[1].astype(jnp.bfloat16)


def levels(rng, shape, shards, least, largest):
    loudness, own = 1.0, jax.random.fold_in(rng, 6)
    for axis_at, blocks in shards:
        heights = jnp.exp(jax.random.uniform(jax.random.fold_in(own, axis_at), (blocks,), jnp.float32, least / len(shards), largest / len(shards)))
        loudness = loudness * jnp.repeat(heights, shape[axis_at] // blocks).reshape([-1 if axis == axis_at else 1 for axis in range(len(shape))])
    return loudness


def bell_draw(own_key, shape, spread, limit, split=(), held_as=jnp.bfloat16):
    entries = spread * jax.random.normal(own_key, shape, jnp.float32)
    if split:
        entries = entries * levels(own_key, shape, split, -0.22, 0.18)
    return jnp.clip(entries, -limit, limit).astype(held_as)


def setup_inputs(seed: int = 0) -> dict:
    streams_of = jax.random.split(jax.random.key(seed), 6)
    queries = draw_queries(jax.random.fold_in(streams_of[5], 71), 0)
    key_cells = draw_key_cells(jax.random.fold_in(streams_of[5], 71), 0)
    value_cells = bell_draw(streams_of[2], (NLAT, NLON, FEAT), 1.0, 5.0, ((0, 16), (1, 32)))
    grad_output = bell_draw(streams_of[3], (NLAT, NLON, FEAT), 1.0, 5.0, ((0, 16), (1, 32)))
    rel_bias = bell_draw(streams_of[4], (HEADS, SPAN * SPAN), 1.0, 4.0, (), jnp.float32)
    return {"queries": queries, "key_cells": key_cells, "value_cells": value_cells, "grad_output": grad_output, "rel_bias": rel_bias}


HIGH = lax.Precision.HIGHEST


def offset_onehot(inner_len, outer_len, span_len, direction, offset):
    shape_all = (inner_len, outer_len, span_len)
    offset_index = lax.broadcasted_iota(jnp.int32, shape_all, 2)
    inner_index = lax.broadcasted_iota(jnp.int32, shape_all, 0)
    outer_index = lax.broadcasted_iota(jnp.int32, shape_all, 1)
    return (offset_index == direction * (outer_index - inner_index) + offset).astype(jnp.float32)


def expand_bias(rel_bias, direction, offset):
    span_len = 2 * RADIUS + 1
    extent = TILE + 2 * RADIUS
    head_count = rel_bias.shape[0]
    offsets_table = rel_bias.reshape(head_count, span_len, span_len)
    onehot = offset_onehot(TILE, extent, span_len, direction, offset)
    partial_sum = jnp.einsum("hab,jcb->hajc", offsets_table, onehot, precision=HIGH)
    expanded = jnp.einsum("ira,hajc->hijrc", onehot, partial_sum, precision=HIGH)
    inside = jnp.einsum("ira,jcb->ijrc", onehot, onehot, precision=HIGH) > 0.5
    return expanded.reshape(head_count, TILE * TILE, extent * extent), inside.reshape(TILE * TILE, extent * extent)


def wrap_pad(values):
    widened = jnp.concatenate([values[:, -RADIUS:], values, values[:, :RADIUS]], axis=1)
    return jnp.pad(widened, ((RADIUS, RADIUS), (0, 0), (0, 0)))


def strip_blocks(padded, first_row):
    extent = TILE + 2 * RADIUS
    strip = lax.dynamic_slice_in_dim(padded, first_row, extent, 0)
    starts = jnp.arange(NLON // TILE, dtype=jnp.int32) * TILE
    columns = starts[:, None] + jnp.arange(extent, dtype=jnp.int32)[None, :]
    picked = strip[:, columns]
    return picked.transpose(1, 0, 2, 3).reshape(NLON // TILE, extent * extent, padded.shape[-1])


def row_tiles(values, first_row):
    band = lax.dynamic_slice_in_dim(values, first_row, TILE, 0)
    arranged = band.reshape(TILE, NLON // TILE, TILE, values.shape[-1]).transpose(1, 0, 2, 3)
    return arranged.reshape(NLON // TILE, TILE * TILE, values.shape[-1])


def untile(stacked):
    channels = stacked.shape[-1]
    arranged = stacked.reshape(NLAT // TILE, NLON // TILE, TILE, TILE, channels).transpose(0, 2, 1, 3, 4)
    return arranged.reshape(NLAT, NLON, channels)


def rounded(values):
    return lax.optimization_barrier(values.astype(jnp.bfloat16)).astype(jnp.float32)


def split_heads(values):
    return values.astype(jnp.float32).reshape(values.shape[0], values.shape[1], HEADS, HEAD_DIM)


def band_inside(first_row):
    extent = TILE + 2 * RADIUS
    global_row = first_row - RADIUS + jnp.arange(extent, dtype=jnp.int32)
    inside = (global_row >= 0) & (global_row < NLAT)
    return jnp.broadcast_to(inside[:, None], (extent, extent)).reshape(extent * extent)


def reference(queries, key_cells, value_cells, grad_output, rel_bias):
    factor = HEAD_DIM ** -0.5
    bias_query, inside_query = expand_bias(rel_bias, 1, 0)
    bias_key, inside_key = expand_bias(rel_bias, -1, 2 * RADIUS)
    key_pad = wrap_pad(key_cells)
    value_pad = wrap_pad(value_cells)
    starts = jnp.arange(NLAT // TILE, dtype=jnp.int32) * TILE

    def query_band(first_row):
        query_heads = split_heads(row_tiles(queries, first_row))
        grad_heads = split_heads(row_tiles(grad_output, first_row))
        key_heads = split_heads(strip_blocks(key_pad, first_row))
        value_heads = split_heads(strip_blocks(value_pad, first_row))
        allowed = inside_query & band_inside(first_row)[None, :]
        scores = jnp.einsum("tqhd,tkhd->thqk", query_heads, key_heads) * factor + bias_query[None]
        scores = jnp.where(allowed[None, None], scores, -jnp.inf)
        row_max = jnp.max(scores, axis=-1, keepdims=True)
        log_total = row_max + jnp.log(jnp.sum(jnp.exp(scores - row_max), axis=-1, keepdims=True))
        probability = jnp.exp(scores - log_total)
        weights = rounded(probability)
        attended = jnp.einsum("thqk,tkhd->tqhd", weights, value_heads)
        row_dot = jnp.sum(grad_heads * attended, axis=-1)
        grad_prob = jnp.einsum("tqhd,tkhd->thqk", grad_heads, value_heads)
        dscore = rounded(probability * (grad_prob - jnp.transpose(row_dot, (0, 2, 1))[..., None]))
        grad_q = jnp.einsum("thqk,tkhd->tqhd", dscore, key_heads) * factor
        tile_count = attended.shape[0]
        return (attended.reshape(tile_count, TILE * TILE, HEADS * HEAD_DIM).astype(jnp.bfloat16),
                grad_q.reshape(tile_count, TILE * TILE, HEADS * HEAD_DIM).astype(jnp.bfloat16),
                jnp.transpose(log_total[..., 0], (0, 2, 1)), row_dot)

    out_tiles, grad_q_tiles, total_tiles, dot_tiles = lax.map(query_band, starts)
    summary = jnp.concatenate([untile(total_tiles), untile(dot_tiles)], axis=-1)
    query_pad = wrap_pad(queries)
    grad_pad = wrap_pad(grad_output)
    summary_pad = wrap_pad(summary)

    def key_band(first_row):
        key_heads = split_heads(row_tiles(key_cells, first_row))
        value_heads = split_heads(row_tiles(value_cells, first_row))
        query_heads = split_heads(strip_blocks(query_pad, first_row))
        grad_heads = split_heads(strip_blocks(grad_pad, first_row))
        nearby = strip_blocks(summary_pad, first_row)
        totals = jnp.transpose(nearby[..., :HEADS], (0, 2, 1))[:, :, None, :]
        dots = jnp.transpose(nearby[..., HEADS:], (0, 2, 1))[:, :, None, :]
        allowed = inside_key & band_inside(first_row)[None, :]
        scores = jnp.einsum("tkhd,tqhd->thkq", key_heads, query_heads) * factor + bias_key[None]
        scores = jnp.where(allowed[None, None], scores, -jnp.inf)
        probability = jnp.exp(scores - totals)
        weights = rounded(probability)
        grad_prob = jnp.einsum("tkhd,tqhd->thkq", value_heads, grad_heads)
        dscore = rounded(probability * (grad_prob - dots))
        grad_k = jnp.einsum("thkq,tqhd->tkhd", dscore, query_heads) * factor
        grad_v = jnp.einsum("thkq,tqhd->tkhd", weights, grad_heads)
        tile_count = grad_k.shape[0]
        return (grad_k.reshape(tile_count, TILE * TILE, HEADS * HEAD_DIM).astype(jnp.bfloat16),
                grad_v.reshape(tile_count, TILE * TILE, HEADS * HEAD_DIM).astype(jnp.bfloat16))

    grad_k_tiles, grad_v_tiles = lax.map(key_band, starts)
    return (untile(out_tiles), untile(grad_q_tiles), untile(grad_k_tiles), untile(grad_v_tiles))
```

```python
import jax
import jax.numpy as jnp
from jax import lax
from jax.experimental import pallas as pl
from jax.experimental.pallas import tpu as pltpu
from jax.sharding import PartitionSpec as P

HEAD_DIM = 64
RADIUS = 6
SPAN = 13
MESH = pl.DeviceIdType.MESH
NEG = -1e30

CHUNKS = 4
HEIGHT = 8
BREADTH = 16
SIDE = 48
WEST = 96
EAST = 144
CENTRE = 224
STRIP = 192
NORTH = CENTRE
SOUTH = CENTRE + STRIP
KEYS = CENTRE + 2 * STRIP
ROW_AT = [0, 16, 32, 48, 64, 80, 192, 208]


def side_groups(base, kind):
    return [(base + t, base + 6 + t // 3, kind + t % 3) for t in range(6)]


def row_groups(base, rows):
    return [(base + r, base + r, kind) for r in rows for kind in (0, 1)]


def key_groups():
    def sides(base):
        return side_groups(base, 2) + side_groups(base, 5)

    centre = row_groups(0, range(6)) + sides(0) + row_groups(0, (6, 7))
    north = row_groups(-8, range(2, 6)) + sides(-8) + row_groups(-8, (6, 7))
    south = row_groups(8, range(6)) + sides(8)
    return [(g, 0) for g in centre] + [(g, 1) for g in north] + [(g, 2) for g in south]


def slot_iota():
    return lax.broadcasted_iota(jnp.int32, (8, 128), 0)


def offset_index(kind):
    slot = slot_iota()
    lane = lax.broadcasted_iota(jnp.int32, (8, 128), 1)
    row, col = lane // BREADTH, lane % BREADTH
    if kind < 2:
        cell = slot + 8 * kind
    else:
        first = -RADIUS if kind < 5 else BREADTH
        cell = jnp.where(slot < 6, first + slot, first + 2 * ((kind - 2) % 3) + slot - 6)
    f = cell - col + RADIUS
    return jnp.where((f >= 0) & (f < SPAN), (HEIGHT - 1 - row) * SPAN + f, 127)


def dot(a, b, on_a, on_b):
    return lax.dot_general(
        a, b, (((on_a,), (on_b,)), ((), ())), preferred_element_type=jnp.float32
    )


def kernel(
    q_ref, k_ref, v_ref, g_ref, rel_ref, o_ref, dq_ref, dk_ref, dv_ref,
    cells, edges, bias, table, padded, strips_out, strips_in, centre, sides_out, sides_in,
    lon_s, lon_r, lat_s, lat_r, rlat_s, rlat_r, rlon_s, rlon_r,
):
    lat, lon = lax.axis_index("lat"), lax.axis_index("lon")
    n_lat, n_lon = lax.axis_size("lat"), lax.axis_size("lon")
    west = (lat, lax.rem(lon + n_lon - 1, n_lon))
    east = (lat, lax.rem(lon + 1, n_lon))
    north = (lat - 1, lon)
    south = (lat + 1, lon)
    has_north, has_south = lat > 0, lat < n_lat - 1
    factor = HEAD_DIM**-0.5
    slot = slot_iota()

    barrier = pltpu.get_barrier_semaphore()
    for side in (west, east):
        pl.semaphore_signal(barrier, inc=1, device_id=side, device_id_type=MESH)

    @pl.when(has_north)
    def _():
        pl.semaphore_signal(barrier, inc=1, device_id=north, device_id_type=MESH)

    @pl.when(has_south)
    def _():
        pl.semaphore_signal(barrier, inc=1, device_id=south, device_id_type=MESH)

    def lanes(g):
        return pl.ds(128 * g, 128)

    for g in range(CHUNKS):
        for a, ref in ((0, k_ref), (1, v_ref)):
            block = ref[:, lanes(g)]
            cells[g, a, 0:96] = block[0:96]
            cells[g, a, 192:224] = block[96:128]
            wide = block.astype(jnp.float32)
            low = [wide[16 * r : 16 * r + 8] for r in range(8)]
            high = [wide[16 * r + 8 : 16 * r + 16] for r in range(8)]
            to_west, to_east = [], []
            for t in range(6):
                j, last = 2 * (t % 3), 6 + t // 3
                spare = low[last] if j == 6 else pltpu.roll(low[last], 6 - j, 0)
                to_west.append(jnp.where(slot < 6, low[t], spare))
                spare = high[last] if j == 4 else pltpu.roll(high[last], 4 - j, 0)
                to_east.append(jnp.where(slot < 6, pltpu.roll(high[t], 6, 0), spare))
            edges[g, 0, a] = jnp.concatenate(to_west, axis=0).astype(jnp.bfloat16)
            edges[g, 1, a] = jnp.concatenate(to_east, axis=0).astype(jnp.bfloat16)

    pl.semaphore_wait(barrier, 2 + has_north.astype(jnp.int32) + has_south.astype(jnp.int32))

    def remote(src, dst, sends, recvs, g, way, target):
        return pltpu.make_async_remote_copy(
            src_ref=src, dst_ref=dst, send_sem=sends.at[g, way], recv_sem=recvs.at[g, way],
            device_id=target, device_id_type=MESH,
        )

    def lon_copies(g):
        return [
            remote(edges.at[g, 0], cells.at[g, :, pl.ds(EAST, SIDE)], lon_s, lon_r, g, 0, west),
            remote(edges.at[g, 1], cells.at[g, :, pl.ds(WEST, SIDE)], lon_s, lon_r, g, 1, east),
        ]

    def lat_copies(g):
        up = remote(
            cells.at[g, :, pl.ds(0, STRIP)], cells.at[g, :, pl.ds(SOUTH, STRIP)], lat_s, lat_r, g, 0, north
        )
        down = remote(
            cells.at[g, :, pl.ds(32, STRIP)], cells.at[g, :, pl.ds(NORTH, STRIP)], lat_s, lat_r, g, 1, south
        )
        return up, down

    def back_lat_copies(g):
        up = remote(strips_out.at[g, 0], strips_in.at[g, 0], rlat_s, rlat_r, g, 0, north)
        down = remote(strips_out.at[g, 1], strips_in.at[g, 1], rlat_s, rlat_r, g, 1, south)
        return up, down

    def back_lon_copies(g):
        return [
            remote(sides_out.at[g, 0], sides_in.at[g, 0], rlon_s, rlon_r, g, 0, west),
            remote(sides_out.at[g, 1], sides_in.at[g, 1], rlon_s, rlon_r, g, 1, east),
        ]

    def start_pair(copies):
        up, down = copies

        @pl.when(has_north)
        def _():
            up.start()

        @pl.when(has_south)
        def _():
            down.start()

    def wait_pair(copies):
        up, down = copies

        @pl.when(has_south)
        def _():
            up.wait_recv()

        @pl.when(has_north)
        def _():
            down.wait_recv()

    for g in range(CHUNKS):
        for copy in lon_copies(g):
            copy.start()

    for g in range(CHUNKS):

        @pl.when(jnp.logical_not(has_north))
        def _():
            cells[g, :, NORTH : NORTH + STRIP] = jnp.zeros((2, STRIP, 128), jnp.bfloat16)

        @pl.when(jnp.logical_not(has_south))
        def _():
            cells[g, :, SOUTH : SOUTH + STRIP] = jnp.zeros((2, STRIP, 128), jnp.bfloat16)

    padded[...] = jnp.full(padded.shape, NEG, jnp.float32)
    padded[:, 128 : 128 + SPAN * SPAN] = rel_ref[...]
    line = padded[...]
    lane = lax.broadcasted_iota(jnp.int32, (8, 128), 1)
    for c in range(-8, 16):
        first = 128 + SPAN * (c - 1)
        rolled = pltpu.roll(line, 512 - first, 1)[:, :128]
        table[c + 8] = jnp.where(lane < 8 * SPAN, rolled, NEG)

    indices = [offset_index(kind) for kind in range(8)]
    outside = [
        None,
        jnp.where(has_north, 0.0, NEG).astype(jnp.float32),
        jnp.where(has_south, 0.0, NEG).astype(jnp.float32),
    ]

    def fill_bias(pair, carry):
        for half in range(2):
            head = 2 * pair + half
            rows = {}

            def row(c):
                if c not in rows:
                    rows[c] = jnp.broadcast_to(table[c + 8, pl.ds(head, 1), :], (8, 128))
                return rows[c]

            for i, ((c, spare, kind), region) in enumerate(key_groups()):
                source = row(c) if c == spare else jnp.where(slot < 6, row(c), row(spare))
                value = jnp.take_along_axis(source, indices[kind], axis=1)
                if outside[region] is not None:
                    value = value + outside[region]
                bias[pair, 8 * i : 8 * i + 8, 128 * half : 128 * half + 128] = value
        return carry

    lax.fori_loop(0, CHUNKS, fill_bias, 0)

    left = lax.broadcasted_iota(jnp.int32, (128, 128), 1) < HEAD_DIM
    top = lax.broadcasted_iota(jnp.int32, (128, 128), 0) < HEAD_DIM

    def by_head(block):
        wide = block.astype(jnp.float32)
        both = jnp.concatenate([jnp.where(left, wide, 0.0), jnp.where(left, 0.0, wide)], axis=0)
        return both.astype(jnp.bfloat16)

    def from_heads(found):
        return jnp.where(top, found[:, :128], found[:, 128:]).T

    def forward_strips(g):
        for copy in lon_copies(g):
            copy.wait_recv()
        start_pair(lat_copies(g))

    def attend(g):
        wait_pair(lat_copies(g))
        queries, grads = by_head(q_ref[:, lanes(g)]), by_head(g_ref[:, lanes(g)])
        keys, values = cells[g, 0], cells[g, 1]
        scores = dot(keys, queries, 1, 1) * factor + bias[g]
        row_max = jnp.max(scores, axis=0, keepdims=True)
        raised = jnp.exp(scores - row_max)
        probability = raised * (1.0 / jnp.sum(raised, axis=0, keepdims=True))
        weights = probability.astype(jnp.bfloat16)
        grad_prob = dot(values, grads, 1, 1)
        row_dot = jnp.sum(weights.astype(jnp.float32) * grad_prob, axis=0, keepdims=True)
        dscore = (probability * (grad_prob - row_dot)).astype(jnp.bfloat16)
        grad_v = dot(weights, grads, 1, 0)
        grad_k = dot(dscore, queries, 1, 0) * factor
        for a, found in ((0, grad_k), (1, grad_v)):
            strips_out[g, 0, a] = found[NORTH : NORTH + STRIP].astype(jnp.bfloat16)
            strips_out[g, 1, a] = found[SOUTH : SOUTH + STRIP].astype(jnp.bfloat16)
            centre[g, a] = found[:CENTRE]
        start_pair(back_lat_copies(g))
        o_ref[:, lanes(g)] = from_heads(dot(values, weights, 0, 0)).astype(jnp.bfloat16)
        grad_q = from_heads(dot(keys, dscore, 0, 0)) * factor
        dq_ref[:, lanes(g)] = grad_q.astype(jnp.bfloat16)

    def return_sides(g):
        wait_pair(back_lat_copies(g))

        @pl.when(has_south)
        def _():
            for a in range(2):
                centre[g, a, 32:224] += strips_in[g, 0, a].astype(jnp.float32)

        @pl.when(has_north)
        def _():
            for a in range(2):
                centre[g, a, 0:192] += strips_in[g, 1, a].astype(jnp.float32)

        for a in range(2):
            sides_out[g, 0, a] = centre[g, a, WEST : WEST + SIDE].astype(jnp.bfloat16)
            sides_out[g, 1, a] = centre[g, a, EAST : EAST + SIDE].astype(jnp.bfloat16)
        for copy in back_lon_copies(g):
            copy.start()

    def finish(g):
        for copy in back_lon_copies(g):
            copy.wait_recv()
        for a, ref in ((0, dk_ref), (1, dv_ref)):
            from_east = sides_in[g, 0, a].astype(jnp.float32)
            from_west = sides_in[g, 1, a].astype(jnp.float32)
            east_groups = [from_east[8 * t : 8 * t + 8] for t in range(6)]
            west_groups = [from_west[8 * t : 8 * t + 8] for t in range(6)]
            rows = []
            for r in range(8):
                if r < 6:
                    low, high = west_groups[r], pltpu.roll(east_groups[r], 2, 0)
                else:
                    w, e = west_groups[3 * (r - 6) :], east_groups[3 * (r - 6) :]
                    low = jnp.where(
                        slot < 2, pltpu.roll(w[0], 2, 0), jnp.where(slot < 4, pltpu.roll(w[1], 4, 0), pltpu.roll(w[2], 6, 0))
                    )
                    high = jnp.where(
                        slot < 4, pltpu.roll(e[0], 4, 0), jnp.where(slot < 6, pltpu.roll(e[1], 6, 0), e[2])
                    )
                at = ROW_AT[r]
                rows.append(centre[g, a, at : at + 8] + jnp.where(slot < 6, low, 0.0))
                rows.append(centre[g, a, at + 8 : at + 16] + jnp.where(slot >= 2, high, 0.0))
            ref[:, lanes(g)] = jnp.concatenate(rows, axis=0).astype(jnp.bfloat16)

    forward_strips(0)
    forward_strips(1)
    attend(0)
    forward_strips(2)
    return_sides(0)
    attend(1)
    forward_strips(3)
    return_sides(1)
    attend(2)
    return_sides(2)
    attend(3)
    return_sides(3)
    for g in range(CHUNKS):
        finish(g)

    for g in range(CHUNKS):
        for copy in lon_copies(g) + back_lon_copies(g):
            copy.wait_send()
        for up, down in (lat_copies(g), back_lat_copies(g)):

            @pl.when(has_north)
            def _():
                up.wait_send()

            @pl.when(has_south)
            def _():
                down.wait_send()


def shards(queries, key_cells, value_cells, grad_output, rel_bias):
    height, breadth, channels = queries.shape
    flat = [x.reshape(height * breadth, channels) for x in (queries, key_cells, value_cells, grad_output)]
    bf16, f32 = jnp.bfloat16, jnp.float32
    vmem = pl.BlockSpec(memory_space=pltpu.VMEM)
    semaphores = [pltpu.SemaphoreType.DMA((CHUNKS, 2))] * 8
    found = pl.pallas_call(
        kernel,
        out_shape=[jax.ShapeDtypeStruct((height * breadth, channels), bf16)] * 4,
        in_specs=[vmem] * 5,
        out_specs=[vmem] * 4,
        scratch_shapes=[
            pltpu.VMEM((CHUNKS, 2, KEYS, 128), bf16),
            pltpu.VMEM((CHUNKS, 2, 2, SIDE, 128), bf16),
            pltpu.VMEM((CHUNKS, KEYS, 256), f32),
            pltpu.VMEM((24, 8, 128), f32),
            pltpu.VMEM((8, 512), f32),
            pltpu.VMEM((CHUNKS, 2, 2, STRIP, 128), bf16),
            pltpu.VMEM((CHUNKS, 2, 2, STRIP, 128), bf16),
            pltpu.VMEM((CHUNKS, 2, CENTRE, 128), f32),
            pltpu.VMEM((CHUNKS, 2, 2, SIDE, 128), bf16),
            pltpu.VMEM((CHUNKS, 2, 2, SIDE, 128), bf16),
        ]
        + semaphores,
        compiler_params=pltpu.CompilerParams(
            collective_id=0, has_side_effects=True, vmem_limit_bytes=40 * 1024 * 1024
        ),
        name="neighbourhood",
    )(*flat, rel_bias)
    return tuple(x.reshape(height, breadth, channels) for x in found)


def solution(mesh):
    tiled = P("lat", "lon", None)
    return jax.shard_map(
        shards, mesh=mesh, in_specs=(tiled,) * 4 + (P(),), out_specs=(tiled,) * 4, check_vma=False
    )
```

```python
import jax
import jax.numpy as jnp
from jax import lax
from jax.experimental import pallas as pl
from jax.experimental.pallas import tpu as pltpu
from jax.sharding import PartitionSpec as P

HEAD_DIM = 64
RADIUS = 6
SPAN = 13
MESH = pl.DeviceIdType.MESH
NEG = -1e30
LIMIT = 56 * 1000 * 1000

CHUNKS = 4
HEIGHT = 8
BREADTH = 16
SIDE = 48
OWN = 96
WEST = 128
EAST = 176
CENTRE = 224
STRIP = 192
NORTH = CENTRE
SOUTH = CENTRE + STRIP
KEYS = CENTRE + 2 * STRIP


def side_groups(base, kind):
    return [(base + t, base + 6 + t // 3, kind + t % 3) for t in range(6)]


def row_groups(base, rows):
    return [(base + r, base + r, kind) for r in rows for kind in (0, 1)]


def key_groups():
    def sides(base):
        return side_groups(base, 2) + side_groups(base, 5)

    centre = row_groups(0, range(8)) + sides(0)
    north = row_groups(-8, range(2, 8)) + sides(-8)
    south = row_groups(8, range(6)) + sides(8)
    return [(g, 0) for g in centre] + [(g, 1) for g in north] + [(g, 2) for g in south]


def slot_iota():
    return lax.broadcasted_iota(jnp.int32, (8, 128), 0)


def offset_index(kind):
    slot = slot_iota()
    lane = lax.broadcasted_iota(jnp.int32, (8, 128), 1)
    row, col = lane // BREADTH, lane % BREADTH
    if kind < 2:
        cell = slot + 8 * kind
    else:
        first = -RADIUS if kind < 5 else BREADTH
        cell = jnp.where(slot < 6, first + slot, first + 2 * ((kind - 2) % 3) + slot - 6)
    f = cell - col + RADIUS
    return jnp.where((f >= 0) & (f < SPAN), (HEIGHT - 1 - row) * SPAN + f, 127)


def dot(a, b, on_a, on_b):
    return lax.dot_general(
        a, b, (((on_a,), (on_b,)), ((), ())), preferred_element_type=jnp.float32
    )


def kernel(
    q_hbm, k_hbm, v_hbm, g_hbm, rel_hbm, o_hbm, dq_hbm, dk_hbm, dv_hbm,
    o_ref, dq_ref, dk_ref, dv_ref, q_ref, k_ref, v_ref, g_ref, rel_ref, cells, edges, bias, table, padded, strips_out, strips_in, centre, sides_out, sides_in,
    lon_s, lon_r, lat_s, lat_r, rlat_s, rlat_r, rlon_s, rlon_r, own_s, own_r, load_s, store_s,
):
    lat, lon = lax.axis_index("lat"), lax.axis_index("lon")
    n_lat, n_lon = lax.axis_size("lat"), lax.axis_size("lon")
    west = (lat, lax.rem(lon + n_lon - 1, n_lon))
    east = (lat, lax.rem(lon + 1, n_lon))
    north = (lat - 1, lon)
    south = (lat + 1, lon)
    has_north, has_south = lat > 0, lat < n_lat - 1
    factor = HEAD_DIM**-0.5
    slot = slot_iota()

    barrier = pltpu.get_barrier_semaphore()
    for side in (west, east):
        pl.semaphore_signal(barrier, inc=1, device_id=side, device_id_type=MESH)

    @pl.when(has_north)
    def _():
        pl.semaphore_signal(barrier, inc=1, device_id=north, device_id_type=MESH)

    @pl.when(has_south)
    def _():
        pl.semaphore_signal(barrier, inc=1, device_id=south, device_id_type=MESH)

    loads = [
        pltpu.make_async_copy(src, dst, load_s.at[i])
        for i, (src, dst) in enumerate(
            [(k_hbm, k_ref), (v_hbm, v_ref), (rel_hbm, rel_ref), (q_hbm, q_ref), (g_hbm, g_ref)]
        )
    ]
    for load in loads:
        load.start()

    def lanes(g):
        return pl.ds(128 * g, 128)

    def stores(g, which):
        pairs = [(o_ref, o_hbm), (dq_ref, dq_hbm), (dk_ref, dk_hbm), (dv_ref, dv_hbm)]
        return [
            pltpu.make_async_copy(pairs[i][0].at[:, lanes(g)], pairs[i][1].at[:, lanes(g)], store_s.at[i, g])
            for i in which
        ]

    for load in loads[:2]:
        load.wait()

    for g in range(CHUNKS):
        for a, ref in ((0, k_ref), (1, v_ref)):
            block = ref[:, lanes(g)]
            cells[g, a, 0:128] = block
            wide = block.astype(jnp.float32)
            low = [wide[16 * r : 16 * r + 8] for r in range(8)]
            high = [wide[16 * r + 8 : 16 * r + 16] for r in range(8)]
            to_west, to_east = [], []
            for t in range(6):
                j, last = 2 * (t % 3), 6 + t // 3
                spare = low[last] if j == 6 else pltpu.roll(low[last], 6 - j, 0)
                to_west.append(jnp.where(slot < 6, low[t], spare))
                spare = high[last] if j == 4 else pltpu.roll(high[last], 4 - j, 0)
                to_east.append(jnp.where(slot < 6, pltpu.roll(high[t], 6, 0), spare))
            edges[g, 0, a] = jnp.concatenate(to_west, axis=0).astype(jnp.bfloat16)
            edges[g, 1, a] = jnp.concatenate(to_east, axis=0).astype(jnp.bfloat16)

    pl.semaphore_wait(barrier, 2 + has_north.astype(jnp.int32) + has_south.astype(jnp.int32))

    def remote(src, dst, sends, recvs, g, way, target):
        return pltpu.make_async_remote_copy(
            src_ref=src, dst_ref=dst, send_sem=sends.at[g, way], recv_sem=recvs.at[g, way],
            device_id=target, device_id_type=MESH,
        )

    def lon_copies(g):
        return [
            remote(edges.at[g, 0], cells.at[g, :, pl.ds(EAST, SIDE)], lon_s, lon_r, g, 0, west),
            remote(edges.at[g, 1], cells.at[g, :, pl.ds(WEST, SIDE)], lon_s, lon_r, g, 1, east),
        ]

    def own_copies():
        up = remote(cells.at[:, :, pl.ds(0, OWN)], cells.at[:, :, pl.ds(SOUTH, OWN)], own_s, own_r, 0, 0, north)
        down = remote(cells.at[:, :, pl.ds(32, OWN)], cells.at[:, :, pl.ds(NORTH, OWN)], own_s, own_r, 0, 1, south)
        return up, down

    def lat_copies(g):
        sides = cells.at[g, :, pl.ds(WEST, 2 * SIDE)]
        up = remote(sides, cells.at[g, :, pl.ds(SOUTH + OWN, 2 * SIDE)], lat_s, lat_r, g, 0, north)
        down = remote(sides, cells.at[g, :, pl.ds(NORTH + OWN, 2 * SIDE)], lat_s, lat_r, g, 1, south)
        return up, down

    def back_lat_copies(g):
        def copy(way, target):
            part = pl.ds(OWN, 2 * SIDE)
            return remote(strips_out.at[way, g, :, part], strips_in.at[way, g, :, part], rlat_s, rlat_r, g, way, target)

        return copy(0, north), copy(1, south)

    def back_own_copies():
        def copy(way, target):
            part = pl.ds(0, OWN)
            return remote(strips_out.at[way, :, :, part], strips_in.at[way, :, :, part], own_s, own_r, 1, way, target)

        return copy(0, north), copy(1, south)

    def back_lon_copies(g):
        return [
            remote(sides_out.at[g, 0], sides_in.at[g, 0], rlon_s, rlon_r, g, 0, west),
            remote(sides_out.at[g, 1], sides_in.at[g, 1], rlon_s, rlon_r, g, 1, east),
        ]

    def start_pair(copies):
        up, down = copies

        @pl.when(has_north)
        def _():
            up.start()

        @pl.when(has_south)
        def _():
            down.start()

    def wait_pair(copies):
        up, down = copies

        @pl.when(has_south)
        def _():
            up.wait_recv()

        @pl.when(has_north)
        def _():
            down.wait_recv()

    for g in range(CHUNKS):
        for copy in lon_copies(g):
            copy.start()
    start_pair(own_copies())

    for g in range(CHUNKS):

        @pl.when(jnp.logical_not(has_north))
        def _():
            cells[g, :, NORTH : NORTH + STRIP] = jnp.zeros((2, STRIP, 128), jnp.bfloat16)

        @pl.when(jnp.logical_not(has_south))
        def _():
            cells[g, :, SOUTH : SOUTH + STRIP] = jnp.zeros((2, STRIP, 128), jnp.bfloat16)

    for load in loads[2:]:
        load.wait()

    padded[...] = jnp.full(padded.shape, NEG, jnp.float32)
    padded[:, 128 : 128 + SPAN * SPAN] = rel_ref[...]
    line = padded[...]
    lane = lax.broadcasted_iota(jnp.int32, (8, 128), 1)
    for c in range(-8, 16):
        first = 128 + SPAN * (c - 1)
        rolled = pltpu.roll(line, 512 - first, 1)[:, :128]
        table[c + 8] = jnp.where(lane < 8 * SPAN, rolled, NEG)

    indices = [offset_index(kind) for kind in range(8)]
    outside = [
        None,
        jnp.where(has_north, 0.0, NEG).astype(jnp.float32),
        jnp.where(has_south, 0.0, NEG).astype(jnp.float32),
    ]

    def fill_bias(pair, carry):
        for half in range(2):
            head = 2 * pair + half
            rows = {}

            def row(c):
                if c not in rows:
                    rows[c] = jnp.broadcast_to(table[c + 8, pl.ds(head, 1), :], (8, 128))
                return rows[c]

            for i, ((c, spare, kind), region) in enumerate(key_groups()):
                source = row(c) if c == spare else jnp.where(slot < 6, row(c), row(spare))
                value = jnp.take_along_axis(source, indices[kind], axis=1)
                if outside[region] is not None:
                    value = value + outside[region]
                bias[pair, 8 * i : 8 * i + 8, 128 * half : 128 * half + 128] = value
        return carry

    lax.fori_loop(0, CHUNKS, fill_bias, 0)

    left = lax.broadcasted_iota(jnp.int32, (128, 128), 1) < HEAD_DIM
    top = lax.broadcasted_iota(jnp.int32, (128, 128), 0) < HEAD_DIM

    def by_head(block):
        wide = block.astype(jnp.float32)
        both = jnp.concatenate([jnp.where(left, wide, 0.0), jnp.where(left, 0.0, wide)], axis=0)
        return both.astype(jnp.bfloat16)

    def from_heads(found):
        return jnp.where(top, found[:, :128], found[:, 128:]).T

    def forward_strips(g):
        for copy in lon_copies(g):
            copy.wait_recv()
        start_pair(lat_copies(g))

    def attend(g):
        wait_pair(lat_copies(g))
        queries, grads = by_head(q_ref[:, lanes(g)]), by_head(g_ref[:, lanes(g)])
        keys, values = cells[g, 0], cells[g, 1]
        scores = dot(keys, queries, 1, 1) * factor + bias[g]
        row_max = jnp.max(scores, axis=0, keepdims=True)
        raised = jnp.exp(scores - row_max)
        probability = raised * (1.0 / jnp.sum(raised, axis=0, keepdims=True))
        weights = probability.astype(jnp.bfloat16)
        grad_prob = dot(values, grads, 1, 1)
        row_dot = jnp.sum(weights.astype(jnp.float32) * grad_prob, axis=0, keepdims=True)
        dscore = (probability * (grad_prob - row_dot)).astype(jnp.bfloat16)
        grad_v = dot(weights, grads, 1, 0)
        grad_k = dot(dscore, queries, 1, 0) * factor
        for a, found in ((0, grad_k), (1, grad_v)):
            strips_out[0, g, a] = found[NORTH : NORTH + STRIP].astype(jnp.bfloat16)
            strips_out[1, g, a] = found[SOUTH : SOUTH + STRIP].astype(jnp.bfloat16)
            centre[g, a] = found[:CENTRE]
        start_pair(back_lat_copies(g))
        o_ref[:, lanes(g)] = from_heads(dot(values, weights, 0, 0)).astype(jnp.bfloat16)
        grad_q = from_heads(dot(keys, dscore, 0, 0)) * factor
        dq_ref[:, lanes(g)] = grad_q.astype(jnp.bfloat16)
        for store in stores(g, (0, 1)):
            store.start()

    def return_sides(g):
        wait_pair(back_lat_copies(g))

        @pl.when(has_south)
        def _():
            for a in range(2):
                centre[g, a, WEST:CENTRE] += strips_in[0, g, a, OWN:STRIP].astype(jnp.float32)

        @pl.when(has_north)
        def _():
            for a in range(2):
                centre[g, a, WEST:CENTRE] += strips_in[1, g, a, OWN:STRIP].astype(jnp.float32)

        for a in range(2):
            sides_out[g, 0, a] = centre[g, a, WEST : WEST + SIDE].astype(jnp.bfloat16)
            sides_out[g, 1, a] = centre[g, a, EAST : EAST + SIDE].astype(jnp.bfloat16)
        for copy in back_lon_copies(g):
            copy.start()

    def finish(g):
        for copy in back_lon_copies(g):
            copy.wait_recv()
        for a, ref in ((0, dk_ref), (1, dv_ref)):
            from_east = sides_in[g, 0, a].astype(jnp.float32)
            from_west = sides_in[g, 1, a].astype(jnp.float32)
            east_groups = [from_east[8 * t : 8 * t + 8] for t in range(6)]
            west_groups = [from_west[8 * t : 8 * t + 8] for t in range(6)]
            rows = []
            for r in range(8):
                if r < 6:
                    low, high = west_groups[r], pltpu.roll(east_groups[r], 2, 0)
                else:
                    w, e = west_groups[3 * (r - 6) :], east_groups[3 * (r - 6) :]
                    low = jnp.where(
                        slot < 2, pltpu.roll(w[0], 2, 0), jnp.where(slot < 4, pltpu.roll(w[1], 4, 0), pltpu.roll(w[2], 6, 0))
                    )
                    high = jnp.where(
                        slot < 4, pltpu.roll(e[0], 4, 0), jnp.where(slot < 6, pltpu.roll(e[1], 6, 0), e[2])
                    )
                at = 16 * r
                rows.append(centre[g, a, at : at + 8] + jnp.where(slot < 6, low, 0.0))
                rows.append(centre[g, a, at + 8 : at + 16] + jnp.where(slot >= 2, high, 0.0))
            ref[:, lanes(g)] = jnp.concatenate(rows, axis=0).astype(jnp.bfloat16)
        for store in stores(g, (2, 3)):
            store.start()

    wait_pair(own_copies())
    forward_strips(0)
    forward_strips(1)
    forward_strips(2)
    attend(0)
    forward_strips(3)
    for g in range(1, CHUNKS):
        attend(g)
    start_pair(back_own_copies())
    for g in range(CHUNKS):
        return_sides(g)

    wait_pair(back_own_copies())

    @pl.when(has_south)
    def _():
        for g in range(CHUNKS):
            for a in range(2):
                centre[g, a, 32:128] += strips_in[0, g, a, 0:OWN].astype(jnp.float32)

    @pl.when(has_north)
    def _():
        for g in range(CHUNKS):
            for a in range(2):
                centre[g, a, 0:96] += strips_in[1, g, a, 0:OWN].astype(jnp.float32)

    for g in range(CHUNKS):
        finish(g)

    def wait_sent(copies):
        up, down = copies

        @pl.when(has_north)
        def _():
            up.wait_send()

        @pl.when(has_south)
        def _():
            down.wait_send()

    wait_sent(own_copies())
    wait_sent(back_own_copies())
    for g in range(CHUNKS):
        for copy in lon_copies(g) + back_lon_copies(g):
            copy.wait_send()
        wait_sent(lat_copies(g))
        wait_sent(back_lat_copies(g))
        for store in stores(g, range(4)):
            store.wait()


def write(*refs):
    sources, targets, sems = refs[:4], refs[4:8], refs[8]
    copies = [pltpu.make_async_copy(s, t, sems.at[i]) for i, (s, t) in enumerate(zip(sources, targets))]
    for copy in copies:
        copy.start()
    for copy in copies:
        copy.wait()


def shards(queries, key_cells, value_cells, grad_output, rel_bias):
    height, breadth, channels = queries.shape
    count = height * breadth
    flat = [x.reshape(count, channels) for x in (queries, key_cells, value_cells, grad_output)]
    bf16, f32 = jnp.bfloat16, jnp.float32
    hbm = pl.BlockSpec(memory_space=pltpu.HBM)
    shapes = [jax.ShapeDtypeStruct((count, channels), bf16)] * 4
    found = pl.pallas_call(
        kernel,
        out_shape=shapes,
        in_specs=[hbm] * 5,
        out_specs=[hbm] * 4,
        scratch_shapes=[pltpu.VMEM((count, channels), bf16)] * 8
        + [
            pltpu.VMEM(rel_bias.shape, f32),
            pltpu.VMEM((CHUNKS, 2, KEYS, 128), bf16),
            pltpu.VMEM((CHUNKS, 2, 2, SIDE, 128), bf16),
            pltpu.VMEM((CHUNKS, KEYS, 256), f32),
            pltpu.VMEM((24, 8, 128), f32),
            pltpu.VMEM((8, 512), f32),
            pltpu.VMEM((2, CHUNKS, 2, STRIP, 128), bf16),
            pltpu.VMEM((2, CHUNKS, 2, STRIP, 128), bf16),
            pltpu.VMEM((CHUNKS, 2, CENTRE, 128), f32),
            pltpu.VMEM((CHUNKS, 2, 2, SIDE, 128), bf16),
            pltpu.VMEM((CHUNKS, 2, 2, SIDE, 128), bf16),
        ]
        + [pltpu.SemaphoreType.DMA((CHUNKS, 2))] * 8
        + [pltpu.SemaphoreType.DMA((2, 2))] * 2
        + [pltpu.SemaphoreType.DMA((5,)), pltpu.SemaphoreType.DMA((4, CHUNKS))],
        compiler_params=pltpu.CompilerParams(
            collective_id=0, has_side_effects=True, vmem_limit_bytes=LIMIT
        ),
        name="neighbourhood",
    )(*flat, rel_bias)
    found = pl.pallas_call(
        write,
        out_shape=shapes,
        in_specs=[hbm] * 4,
        out_specs=[hbm] * 4,
        scratch_shapes=[pltpu.SemaphoreType.DMA((4,))],
        compiler_params=pltpu.CompilerParams(vmem_limit_bytes=LIMIT),
        name="write",
    )(*found)
    return tuple(x.reshape(height, breadth, channels) for x in found)


def solution(mesh):
    tiled = P("lat", "lon", None)
    return jax.shard_map(
        shards, mesh=mesh, in_specs=(tiled,) * 4 + (P(),), out_specs=(tiled,) * 4, check_vma=False
    )
```

```python
import jax
import jax.numpy as jnp
from jax import lax
from jax.experimental import pallas as pl
from jax.experimental.pallas import tpu as pltpu
from jax.sharding import PartitionSpec as P

HEAD_DIM = 64
RADIUS = 6
SPAN = 13
MESH = pl.DeviceIdType.MESH
NEG = -1e30
LIMIT = 40 * 1024 * 1024

CHUNKS = 4
HEIGHT = 8
BREADTH = 16
SIDE = 48
OWN = 96
WEST = 128
EAST = 176
CENTRE = 224
STRIP = 192
NORTH = CENTRE
SOUTH = CENTRE + STRIP
KEYS = CENTRE + 2 * STRIP


def side_groups(base, kind):
    return [(base + t, base + 6 + t // 3, kind + t % 3) for t in range(6)]


def row_groups(base, rows):
    return [(base + r, base + r, kind) for r in rows for kind in (0, 1)]


def key_groups():
    def sides(base):
        return side_groups(base, 2) + side_groups(base, 5)

    centre = row_groups(0, range(8)) + sides(0)
    north = row_groups(-8, range(2, 8)) + sides(-8)
    south = row_groups(8, range(6)) + sides(8)
    return [(g, 0) for g in centre] + [(g, 1) for g in north] + [(g, 2) for g in south]


def slot_iota():
    return lax.broadcasted_iota(jnp.int32, (8, 128), 0)


def offset_index(kind):
    slot = slot_iota()
    lane = lax.broadcasted_iota(jnp.int32, (8, 128), 1)
    row, col = lane // BREADTH, lane % BREADTH
    if kind < 2:
        cell = slot + 8 * kind
    else:
        first = -RADIUS if kind < 5 else BREADTH
        cell = jnp.where(slot < 6, first + slot, first + 2 * ((kind - 2) % 3) + slot - 6)
    f = cell - col + RADIUS
    return jnp.where((f >= 0) & (f < SPAN), (HEIGHT - 1 - row) * SPAN + f, 127)


def dot(a, b, on_a, on_b):
    return lax.dot_general(
        a, b, (((on_a,), (on_b,)), ((), ())), preferred_element_type=jnp.float32
    )


def kernel(
    q_hbm, k_hbm, v_hbm, g_hbm, rel_hbm, o_ref, dq_ref, dk_ref, dv_ref,
    q_ref, k_ref, v_ref, g_ref, rel_ref, cells, edges, bias, table, padded, strips_out, strips_in, centre, sides_out, sides_in,
    kept, lon_s, lon_r, lat_s, lat_r, rlat_s, rlat_r, rlon_s, rlon_r, own_s, own_r, load_s,
):
    lat, lon = lax.axis_index("lat"), lax.axis_index("lon")
    n_lat, n_lon = lax.axis_size("lat"), lax.axis_size("lon")
    west = (lat, lax.rem(lon + n_lon - 1, n_lon))
    east = (lat, lax.rem(lon + 1, n_lon))
    north = (lat - 1, lon)
    south = (lat + 1, lon)
    has_north, has_south = lat > 0, lat < n_lat - 1
    factor = HEAD_DIM**-0.5
    slot = slot_iota()

    barrier = pltpu.get_barrier_semaphore()
    for side in (west, east):
        pl.semaphore_signal(barrier, inc=1, device_id=side, device_id_type=MESH)

    @pl.when(has_north)
    def _():
        pl.semaphore_signal(barrier, inc=1, device_id=north, device_id_type=MESH)

    @pl.when(has_south)
    def _():
        pl.semaphore_signal(barrier, inc=1, device_id=south, device_id_type=MESH)

    loads = [
        pltpu.make_async_copy(src, dst, load_s.at[i])
        for i, (src, dst) in enumerate(
            [(k_hbm, k_ref), (v_hbm, v_ref), (rel_hbm, rel_ref), (q_hbm, q_ref), (g_hbm, g_ref)]
        )
    ]
    for load in loads:
        load.start()

    def lanes(g):
        return pl.ds(128 * g, 128)

    for load in loads[:2]:
        load.wait()

    for g in range(CHUNKS):
        for a, ref in ((0, k_ref), (1, v_ref)):
            block = ref[:, lanes(g)]
            cells[g, a, 0:128] = block
            wide = block.astype(jnp.float32)
            low = [wide[16 * r : 16 * r + 8] for r in range(8)]
            high = [wide[16 * r + 8 : 16 * r + 16] for r in range(8)]
            to_west, to_east = [], []
            for t in range(6):
                j, last = 2 * (t % 3), 6 + t // 3
                spare = low[last] if j == 6 else pltpu.roll(low[last], 6 - j, 0)
                to_west.append(jnp.where(slot < 6, low[t], spare))
                spare = high[last] if j == 4 else pltpu.roll(high[last], 4 - j, 0)
                to_east.append(jnp.where(slot < 6, pltpu.roll(high[t], 6, 0), spare))
            edges[g, 0, a] = jnp.concatenate(to_west, axis=0).astype(jnp.bfloat16)
            edges[g, 1, a] = jnp.concatenate(to_east, axis=0).astype(jnp.bfloat16)

    pl.semaphore_wait(barrier, 2 + has_north.astype(jnp.int32) + has_south.astype(jnp.int32))

    def remote(src, dst, sends, recvs, g, way, target):
        return pltpu.make_async_remote_copy(
            src_ref=src, dst_ref=dst, send_sem=sends.at[g, way], recv_sem=recvs.at[g, way],
            device_id=target, device_id_type=MESH,
        )

    def lon_copies(g):
        return [
            remote(edges.at[g, 0], cells.at[g, :, pl.ds(EAST, SIDE)], lon_s, lon_r, g, 0, west),
            remote(edges.at[g, 1], cells.at[g, :, pl.ds(WEST, SIDE)], lon_s, lon_r, g, 1, east),
        ]

    def own_copies():
        up = remote(cells.at[:, :, pl.ds(0, OWN)], cells.at[:, :, pl.ds(SOUTH, OWN)], own_s, own_r, 0, 0, north)
        down = remote(cells.at[:, :, pl.ds(32, OWN)], cells.at[:, :, pl.ds(NORTH, OWN)], own_s, own_r, 0, 1, south)
        return up, down

    def lat_copies(g):
        sides = cells.at[g, :, pl.ds(WEST, 2 * SIDE)]
        up = remote(sides, cells.at[g, :, pl.ds(SOUTH + OWN, 2 * SIDE)], lat_s, lat_r, g, 0, north)
        down = remote(sides, cells.at[g, :, pl.ds(NORTH + OWN, 2 * SIDE)], lat_s, lat_r, g, 1, south)
        return up, down

    def back_lat_copies(g):
        def copy(way, target):
            part = pl.ds(OWN, 2 * SIDE)
            return remote(strips_out.at[way, g, :, part], strips_in.at[way, g, :, part], rlat_s, rlat_r, g, way, target)

        return copy(0, north), copy(1, south)

    def back_own_copies():
        def copy(way, target):
            part = pl.ds(0, OWN)
            return remote(strips_out.at[way, :, :, part], strips_in.at[way, :, :, part], own_s, own_r, 1, way, target)

        return copy(0, north), copy(1, south)

    def back_lon_copies(g):
        return [
            remote(sides_out.at[g, 0], sides_in.at[g, 0], rlon_s, rlon_r, g, 0, west),
            remote(sides_out.at[g, 1], sides_in.at[g, 1], rlon_s, rlon_r, g, 1, east),
        ]

    def start_pair(copies):
        up, down = copies

        @pl.when(has_north)
        def _():
            up.start()

        @pl.when(has_south)
        def _():
            down.start()

    def wait_pair(copies):
        up, down = copies

        @pl.when(has_south)
        def _():
            up.wait_recv()

        @pl.when(has_north)
        def _():
            down.wait_recv()

    for g in range(CHUNKS):
        for copy in lon_copies(g):
            copy.start()
    start_pair(own_copies())

    for g in range(CHUNKS):

        @pl.when(jnp.logical_not(has_north))
        def _():
            cells[g, :, NORTH : NORTH + STRIP] = jnp.zeros((2, STRIP, 128), jnp.bfloat16)

        @pl.when(jnp.logical_not(has_south))
        def _():
            cells[g, :, SOUTH : SOUTH + STRIP] = jnp.zeros((2, STRIP, 128), jnp.bfloat16)

    for load in loads[2:]:
        load.wait()

    padded[...] = jnp.full(padded.shape, NEG, jnp.float32)
    padded[:, 128 : 128 + SPAN * SPAN] = rel_ref[...]
    line = padded[...]
    lane = lax.broadcasted_iota(jnp.int32, (8, 128), 1)
    for c in range(-8, 16):
        first = 128 + SPAN * (c - 1)
        rolled = pltpu.roll(line, 512 - first, 1)[:, :128]
        table[c + 8] = jnp.where(lane < 8 * SPAN, rolled, NEG)

    indices = [offset_index(kind) for kind in range(8)]
    outside = [
        None,
        jnp.where(has_north, 0.0, NEG).astype(jnp.float32),
        jnp.where(has_south, 0.0, NEG).astype(jnp.float32),
    ]

    def fill_bias(pair, carry):
        for half in range(2):
            head = 2 * pair + half
            rows = {}

            def row(c):
                if c not in rows:
                    rows[c] = jnp.broadcast_to(table[c + 8, pl.ds(head, 1), :], (8, 128))
                return rows[c]

            for i, ((c, spare, kind), region) in enumerate(key_groups()):
                source = row(c) if c == spare else jnp.where(slot < 6, row(c), row(spare))
                value = jnp.take_along_axis(source, indices[kind], axis=1)
                if outside[region] is not None:
                    value = value + outside[region]
                bias[pair, 8 * i : 8 * i + 8, 128 * half : 128 * half + 128] = value
        return carry

    lax.fori_loop(0, CHUNKS, fill_bias, 0)

    left = lax.broadcasted_iota(jnp.int32, (128, 128), 1) < HEAD_DIM
    top = lax.broadcasted_iota(jnp.int32, (128, 128), 0) < HEAD_DIM

    def by_head(block):
        wide = block.astype(jnp.float32)
        both = jnp.concatenate([jnp.where(left, wide, 0.0), jnp.where(left, 0.0, wide)], axis=0)
        return both.astype(jnp.bfloat16)

    def from_heads(found):
        return jnp.where(top, found[:, :128], found[:, 128:]).T

    def forward_strips(g):
        for copy in lon_copies(g):
            copy.wait_recv()
        start_pair(lat_copies(g))

    def attend(g):
        wait_pair(lat_copies(g))
        queries, grads = by_head(q_ref[:, lanes(g)]), by_head(g_ref[:, lanes(g)])
        keys, values = cells[g, 0], cells[g, 1]
        scores = dot(keys, queries, 1, 1) * factor + bias[g]
        row_max = jnp.max(scores, axis=0, keepdims=True)
        raised = jnp.exp(scores - row_max)
        probability = raised * (1.0 / jnp.sum(raised, axis=0, keepdims=True))
        weights = probability.astype(jnp.bfloat16)
        grad_prob = dot(values, grads, 1, 1)
        row_dot = jnp.sum(weights.astype(jnp.float32) * grad_prob, axis=0, keepdims=True)
        dscore = (probability * (grad_prob - row_dot)).astype(jnp.bfloat16)
        grad_v = dot(weights, grads, 1, 0)
        grad_k = dot(dscore, queries, 1, 0) * factor
        for a, found in ((0, grad_k), (1, grad_v)):
            strips_out[0, g, a] = found[NORTH : NORTH + STRIP].astype(jnp.bfloat16)
            strips_out[1, g, a] = found[SOUTH : SOUTH + STRIP].astype(jnp.bfloat16)
            centre[g, a] = found[:CENTRE]
        start_pair(back_lat_copies(g))
        kept[g, 0] = weights
        kept[g, 1] = dscore

    def outputs(g):
        o_ref[:, lanes(g)] = from_heads(dot(cells[g, 1], kept[g, 0], 0, 0)).astype(jnp.bfloat16)
        grad_q = from_heads(dot(cells[g, 0], kept[g, 1], 0, 0)) * factor
        dq_ref[:, lanes(g)] = grad_q.astype(jnp.bfloat16)

    def return_sides(g):
        wait_pair(back_lat_copies(g))

        @pl.when(has_south)
        def _():
            for a in range(2):
                centre[g, a, WEST:CENTRE] += strips_in[0, g, a, OWN:STRIP].astype(jnp.float32)

        @pl.when(has_north)
        def _():
            for a in range(2):
                centre[g, a, WEST:CENTRE] += strips_in[1, g, a, OWN:STRIP].astype(jnp.float32)

        for a in range(2):
            sides_out[g, 0, a] = centre[g, a, WEST : WEST + SIDE].astype(jnp.bfloat16)
            sides_out[g, 1, a] = centre[g, a, EAST : EAST + SIDE].astype(jnp.bfloat16)
        for copy in back_lon_copies(g):
            copy.start()

    def finish(g):
        for copy in back_lon_copies(g):
            copy.wait_recv()
        for a, ref in ((0, dk_ref), (1, dv_ref)):
            from_east = sides_in[g, 0, a].astype(jnp.float32)
            from_west = sides_in[g, 1, a].astype(jnp.float32)
            east_groups = [from_east[8 * t : 8 * t + 8] for t in range(6)]
            west_groups = [from_west[8 * t : 8 * t + 8] for t in range(6)]
            rows = []
            for r in range(8):
                if r < 6:
                    low, high = west_groups[r], pltpu.roll(east_groups[r], 2, 0)
                else:
                    w, e = west_groups[3 * (r - 6) :], east_groups[3 * (r - 6) :]
                    low = jnp.where(
                        slot < 2, pltpu.roll(w[0], 2, 0), jnp.where(slot < 4, pltpu.roll(w[1], 4, 0), pltpu.roll(w[2], 6, 0))
                    )
                    high = jnp.where(
                        slot < 4, pltpu.roll(e[0], 4, 0), jnp.where(slot < 6, pltpu.roll(e[1], 6, 0), e[2])
                    )
                at = 16 * r
                rows.append(centre[g, a, at : at + 8] + jnp.where(slot < 6, low, 0.0))
                rows.append(centre[g, a, at + 8 : at + 16] + jnp.where(slot >= 2, high, 0.0))
            ref[:, lanes(g)] = jnp.concatenate(rows, axis=0).astype(jnp.bfloat16)

    wait_pair(own_copies())
    forward_strips(0)
    forward_strips(1)
    forward_strips(2)
    forward_strips(3)
    attend(0)
    attend(1)
    attend(2)
    return_sides(0)
    attend(3)
    return_sides(1)
    return_sides(2)
    return_sides(3)
    start_pair(back_own_copies())
    for g in range(CHUNKS):
        outputs(g)

    wait_pair(back_own_copies())

    @pl.when(has_south)
    def _():
        for g in range(CHUNKS):
            for a in range(2):
                centre[g, a, 32:128] += strips_in[0, g, a, 0:OWN].astype(jnp.float32)

    @pl.when(has_north)
    def _():
        for g in range(CHUNKS):
            for a in range(2):
                centre[g, a, 0:96] += strips_in[1, g, a, 0:OWN].astype(jnp.float32)

    for g in range(CHUNKS):
        finish(g)

    def wait_sent(copies):
        up, down = copies

        @pl.when(has_north)
        def _():
            up.wait_send()

        @pl.when(has_south)
        def _():
            down.wait_send()

    wait_sent(own_copies())
    wait_sent(back_own_copies())
    for g in range(CHUNKS):
        for copy in lon_copies(g) + back_lon_copies(g):
            copy.wait_send()
        wait_sent(lat_copies(g))
        wait_sent(back_lat_copies(g))


def write(*refs):
    sources, targets, sems = refs[:4], refs[4:8], refs[8]
    copies = [pltpu.make_async_copy(s, t, sems.at[i]) for i, (s, t) in enumerate(zip(sources, targets))]
    for copy in copies:
        copy.start()
    for copy in copies:
        copy.wait()


def shards(queries, key_cells, value_cells, grad_output, rel_bias):
    height, breadth, channels = queries.shape
    count = height * breadth
    flat = [x.reshape(count, channels) for x in (queries, key_cells, value_cells, grad_output)]
    bf16, f32 = jnp.bfloat16, jnp.float32
    hbm = pl.BlockSpec(memory_space=pltpu.HBM)
    shapes = [jax.ShapeDtypeStruct((count, channels), bf16)] * 4
    found = pl.pallas_call(
        kernel,
        out_shape=shapes,
        in_specs=[hbm] * 5,
        out_specs=[pl.BlockSpec(memory_space=pltpu.VMEM)] * 4,
        scratch_shapes=[pltpu.VMEM((count, channels), bf16)] * 4
        + [
            pltpu.VMEM(rel_bias.shape, f32),
            pltpu.VMEM((CHUNKS, 2, KEYS, 128), bf16),
            pltpu.VMEM((CHUNKS, 2, 2, SIDE, 128), bf16),
            pltpu.VMEM((CHUNKS, KEYS, 256), f32),
            pltpu.VMEM((24, 8, 128), f32),
            pltpu.VMEM((8, 512), f32),
            pltpu.VMEM((2, CHUNKS, 2, STRIP, 128), bf16),
            pltpu.VMEM((2, CHUNKS, 2, STRIP, 128), bf16),
            pltpu.VMEM((CHUNKS, 2, CENTRE, 128), f32),
            pltpu.VMEM((CHUNKS, 2, 2, SIDE, 128), bf16),
            pltpu.VMEM((CHUNKS, 2, 2, SIDE, 128), bf16),
            pltpu.VMEM((CHUNKS, 2, KEYS, 256), bf16),
        ]
        + [pltpu.SemaphoreType.DMA((CHUNKS, 2))] * 8
        + [pltpu.SemaphoreType.DMA((2, 2))] * 2
        + [pltpu.SemaphoreType.DMA((5,))],
        compiler_params=pltpu.CompilerParams(
            collective_id=0, has_side_effects=True, vmem_limit_bytes=LIMIT
        ),
        name="neighbourhood",
    )(*[pltpu.with_memory_space_constraint(x, pltpu.HBM) for x in flat + [rel_bias]])
    found = pl.pallas_call(
        write,
        out_shape=shapes,
        in_specs=[hbm] * 4,
        out_specs=[hbm] * 4,
        scratch_shapes=[pltpu.SemaphoreType.DMA((4,))],
        compiler_params=pltpu.CompilerParams(vmem_limit_bytes=LIMIT),
        name="write",
    )(*found)
    return tuple(x.reshape(height, breadth, channels) for x in found)


def solution(mesh):
    tiled = P("lat", "lon", None)
    return jax.shard_map(
        shards, mesh=mesh, in_specs=(tiled,) * 4 + (P(),), out_specs=(tiled,) * 4, check_vma=False
    )
```

```python
import jax
import jax.numpy as jnp
from jax import lax
from jax.experimental import pallas as pl
from jax.experimental.pallas import tpu as pltpu
from jax.sharding import PartitionSpec as P

HEAD_DIM = 64
RADIUS = 6
SPAN = 13
MESH = pl.DeviceIdType.MESH
NEG = -1e30
LIMIT = 40 * 1024 * 1024

CHUNKS = 4
HEIGHT = 8
BREADTH = 16
SIDE = 48
OWN = 96
WEST = 128
EAST = 176
CENTRE = 224
STRIP = 192
NORTH = CENTRE
SOUTH = CENTRE + STRIP
KEYS = CENTRE + 2 * STRIP


def side_groups(base, kind):
    return [(base + t, base + 6 + t // 3, kind + t % 3) for t in range(6)]


def row_groups(base, rows):
    return [(base + r, base + r, kind) for r in rows for kind in (0, 1)]


def key_groups():
    def sides(base):
        return side_groups(base, 2) + side_groups(base, 5)

    centre = row_groups(0, range(8)) + sides(0)
    north = row_groups(-8, range(2, 8)) + sides(-8)
    south = row_groups(8, range(6)) + sides(8)
    return [(g, 0) for g in centre] + [(g, 1) for g in north] + [(g, 2) for g in south]


def slot_iota():
    return lax.broadcasted_iota(jnp.int32, (8, 128), 0)


def offset_index(kind):
    slot = slot_iota()
    lane = lax.broadcasted_iota(jnp.int32, (8, 128), 1)
    row, col = lane // BREADTH, lane % BREADTH
    if kind < 2:
        cell = slot + 8 * kind
    else:
        first = -RADIUS if kind < 5 else BREADTH
        cell = jnp.where(slot < 6, first + slot, first + 2 * ((kind - 2) % 3) + slot - 6)
    f = cell - col + RADIUS
    return jnp.where((f >= 0) & (f < SPAN), (HEIGHT - 1 - row) * SPAN + f, 127)


def dot(a, b, on_a, on_b):
    return lax.dot_general(
        a, b, (((on_a,), (on_b,)), ((), ())), preferred_element_type=jnp.float32
    )


def kernel(
    q_hbm, k_hbm, v_hbm, g_hbm, rel_hbm, o_ref, dq_ref, dk_ref, dv_ref,
    q_ref, k_ref, v_ref, g_ref, rel_ref, cells, edges, bias, table, padded, strips_out, strips_in, centre, sides_out, sides_in,
    kept, lon_s, lon_r, lat_s, lat_r, rlat_s, rlat_r, rlon_s, rlon_r, own_s, own_r, load_s,
):
    lat, lon = lax.axis_index("lat"), lax.axis_index("lon")
    n_lat, n_lon = lax.axis_size("lat"), lax.axis_size("lon")
    west = (lat, lax.rem(lon + n_lon - 1, n_lon))
    east = (lat, lax.rem(lon + 1, n_lon))
    north = (lat - 1, lon)
    south = (lat + 1, lon)
    has_north, has_south = lat > 0, lat < n_lat - 1
    factor = HEAD_DIM**-0.5
    slot = slot_iota()

    barrier = pltpu.get_barrier_semaphore()
    for side in (west, east):
        pl.semaphore_signal(barrier, inc=1, device_id=side, device_id_type=MESH)

    @pl.when(has_north)
    def _():
        pl.semaphore_signal(barrier, inc=1, device_id=north, device_id_type=MESH)

    @pl.when(has_south)
    def _():
        pl.semaphore_signal(barrier, inc=1, device_id=south, device_id_type=MESH)

    loads = [
        pltpu.make_async_copy(src, dst, load_s.at[i])
        for i, (src, dst) in enumerate(
            [(k_hbm, k_ref), (v_hbm, v_ref), (rel_hbm, rel_ref), (q_hbm, q_ref), (g_hbm, g_ref)]
        )
    ]
    for load in loads:
        load.start()

    def lanes(g):
        return pl.ds(128 * g, 128)

    for load in loads[:2]:
        load.wait()

    for g in range(CHUNKS):
        for a, ref in ((0, k_ref), (1, v_ref)):
            block = ref[:, lanes(g)]
            cells[g, a, 0:128] = block
            wide = block.astype(jnp.float32)
            low = [wide[16 * r : 16 * r + 8] for r in range(8)]
            high = [wide[16 * r + 8 : 16 * r + 16] for r in range(8)]
            to_west, to_east = [], []
            for t in range(6):
                j, last = 2 * (t % 3), 6 + t // 3
                spare = low[last] if j == 6 else pltpu.roll(low[last], 6 - j, 0)
                to_west.append(jnp.where(slot < 6, low[t], spare))
                spare = high[last] if j == 4 else pltpu.roll(high[last], 4 - j, 0)
                to_east.append(jnp.where(slot < 6, pltpu.roll(high[t], 6, 0), spare))
            edges[g, 0, a] = jnp.concatenate(to_west, axis=0).astype(jnp.bfloat16)
            edges[g, 1, a] = jnp.concatenate(to_east, axis=0).astype(jnp.bfloat16)

    pl.semaphore_wait(barrier, 2 + has_north.astype(jnp.int32) + has_south.astype(jnp.int32))

    def remote(src, dst, sends, recvs, g, way, target):
        return pltpu.make_async_remote_copy(
            src_ref=src, dst_ref=dst, send_sem=sends.at[g, way], recv_sem=recvs.at[g, way],
            device_id=target, device_id_type=MESH,
        )

    def lon_copies(g):
        return [
            remote(edges.at[g, 0], cells.at[g, :, pl.ds(EAST, SIDE)], lon_s, lon_r, g, 0, west),
            remote(edges.at[g, 1], cells.at[g, :, pl.ds(WEST, SIDE)], lon_s, lon_r, g, 1, east),
        ]

    def own_copies():
        up = remote(cells.at[:, :, pl.ds(0, OWN)], cells.at[:, :, pl.ds(SOUTH, OWN)], own_s, own_r, 0, 0, north)
        down = remote(cells.at[:, :, pl.ds(32, OWN)], cells.at[:, :, pl.ds(NORTH, OWN)], own_s, own_r, 0, 1, south)
        return up, down

    def lat_copies(g):
        sides = cells.at[g, :, pl.ds(WEST, 2 * SIDE)]
        up = remote(sides, cells.at[g, :, pl.ds(SOUTH + OWN, 2 * SIDE)], lat_s, lat_r, g, 0, north)
        down = remote(sides, cells.at[g, :, pl.ds(NORTH + OWN, 2 * SIDE)], lat_s, lat_r, g, 1, south)
        return up, down

    def back_lat_copies(g):
        def copy(way, target):
            part = pl.ds(OWN, 2 * SIDE)
            return remote(strips_out.at[way, g, :, part], strips_in.at[way, g, :, part], rlat_s, rlat_r, g, way, target)

        return copy(0, north), copy(1, south)

    def back_own_copies():
        def copy(way, target):
            part = pl.ds(0, OWN)
            return remote(strips_out.at[way, :, :, part], strips_in.at[way, :, :, part], own_s, own_r, 1, way, target)

        return copy(0, north), copy(1, south)

    def back_lon_copies(g):
        return [
            remote(sides_out.at[g, 0], sides_in.at[g, 0], rlon_s, rlon_r, g, 0, west),
            remote(sides_out.at[g, 1], sides_in.at[g, 1], rlon_s, rlon_r, g, 1, east),
        ]

    def start_pair(copies):
        up, down = copies

        @pl.when(has_north)
        def _():
            up.start()

        @pl.when(has_south)
        def _():
            down.start()

    def wait_pair(copies):
        up, down = copies

        @pl.when(has_south)
        def _():
            up.wait_recv()

        @pl.when(has_north)
        def _():
            down.wait_recv()

    for g in range(CHUNKS):
        for copy in lon_copies(g):
            copy.start()
    start_pair(own_copies())

    for g in range(CHUNKS):

        @pl.when(jnp.logical_not(has_north))
        def _():
            cells[g, :, NORTH : NORTH + STRIP] = jnp.zeros((2, STRIP, 128), jnp.bfloat16)

        @pl.when(jnp.logical_not(has_south))
        def _():
            cells[g, :, SOUTH : SOUTH + STRIP] = jnp.zeros((2, STRIP, 128), jnp.bfloat16)

    for load in loads[2:]:
        load.wait()

    padded[...] = jnp.full(padded.shape, NEG, jnp.float32)
    padded[:, 128 : 128 + SPAN * SPAN] = rel_ref[...]
    line = padded[...]
    lane = lax.broadcasted_iota(jnp.int32, (8, 128), 1)
    for c in range(-8, 16):
        first = 128 + SPAN * (c - 1)
        rolled = pltpu.roll(line, 512 - first, 1)[:, :128]
        table[c + 8] = jnp.where(lane < 8 * SPAN, rolled, NEG)

    indices = [offset_index(kind) for kind in range(8)]
    outside = [
        None,
        jnp.where(has_north, 0.0, NEG).astype(jnp.float32),
        jnp.where(has_south, 0.0, NEG).astype(jnp.float32),
    ]

    def fill_bias(pair, carry):
        for half in range(2):
            head = 2 * pair + half
            rows = {}

            def row(c):
                if c not in rows:
                    rows[c] = jnp.broadcast_to(table[c + 8, pl.ds(head, 1), :], (8, 128))
                return rows[c]

            for i, ((c, spare, kind), region) in enumerate(key_groups()):
                source = row(c) if c == spare else jnp.where(slot < 6, row(c), row(spare))
                value = jnp.take_along_axis(source, indices[kind], axis=1)
                if outside[region] is not None:
                    value = value + outside[region]
                bias[pair, 8 * i : 8 * i + 8, 128 * half : 128 * half + 128] = value
        return carry

    lax.fori_loop(0, CHUNKS, fill_bias, 0)

    left = lax.broadcasted_iota(jnp.int32, (128, 128), 1) < HEAD_DIM
    top = lax.broadcasted_iota(jnp.int32, (128, 128), 0) < HEAD_DIM

    def by_head(block):
        wide = block.astype(jnp.float32)
        both = jnp.concatenate([jnp.where(left, wide, 0.0), jnp.where(left, 0.0, wide)], axis=0)
        return both.astype(jnp.bfloat16)

    def from_heads(found):
        return jnp.where(top, found[:, :128], found[:, 128:]).T

    def forward_strips(g):
        for copy in lon_copies(g):
            copy.wait_recv()
        start_pair(lat_copies(g))

    def attend(g):
        wait_pair(lat_copies(g))
        queries, grads = by_head(q_ref[:, lanes(g)]), by_head(g_ref[:, lanes(g)])
        keys, values = cells[g, 0], cells[g, 1]
        scores = dot(keys, queries, 1, 1) * factor + bias[g]
        row_max = jnp.max(scores, axis=0, keepdims=True)
        raised = jnp.exp(scores - row_max)
        probability = raised * (1.0 / jnp.sum(raised, axis=0, keepdims=True))
        weights = probability.astype(jnp.bfloat16)
        grad_prob = dot(values, grads, 1, 1)
        row_dot = jnp.sum(weights.astype(jnp.float32) * grad_prob, axis=0, keepdims=True)
        dscore = (probability * (grad_prob - row_dot)).astype(jnp.bfloat16)
        grad_v = dot(weights, grads, 1, 0)
        grad_k = dot(dscore, queries, 1, 0) * factor
        for a, found in ((0, grad_k), (1, grad_v)):
            strips_out[0, g, a] = found[NORTH : NORTH + STRIP].astype(jnp.bfloat16)
            strips_out[1, g, a] = found[SOUTH : SOUTH + STRIP].astype(jnp.bfloat16)
            centre[g, a] = found[:CENTRE]
        start_pair(back_lat_copies(g))
        kept[g, 0] = weights
        kept[g, 1] = dscore

    def outputs(g):
        o_ref[:, lanes(g)] = from_heads(dot(cells[g, 1], kept[g, 0], 0, 0)).astype(jnp.bfloat16)
        grad_q = from_heads(dot(cells[g, 0], kept[g, 1], 0, 0)) * factor
        dq_ref[:, lanes(g)] = grad_q.astype(jnp.bfloat16)

    def return_sides(g):
        wait_pair(back_lat_copies(g))

        @pl.when(has_south)
        def _():
            for a in range(2):
                centre[g, a, WEST:CENTRE] += strips_in[0, g, a, OWN:STRIP].astype(jnp.float32)

        @pl.when(has_north)
        def _():
            for a in range(2):
                centre[g, a, WEST:CENTRE] += strips_in[1, g, a, OWN:STRIP].astype(jnp.float32)

        for a in range(2):
            sides_out[g, 0, a] = centre[g, a, WEST : WEST + SIDE].astype(jnp.bfloat16)
            sides_out[g, 1, a] = centre[g, a, EAST : EAST + SIDE].astype(jnp.bfloat16)
        for copy in back_lon_copies(g):
            copy.start()

    def finish(g):
        for copy in back_lon_copies(g):
            copy.wait_recv()
        for a, ref in ((0, dk_ref), (1, dv_ref)):
            from_east = sides_in[g, 0, a].astype(jnp.float32)
            from_west = sides_in[g, 1, a].astype(jnp.float32)
            east_groups = [from_east[8 * t : 8 * t + 8] for t in range(6)]
            west_groups = [from_west[8 * t : 8 * t + 8] for t in range(6)]
            rows = []
            for r in range(8):
                if r < 6:
                    low, high = west_groups[r], pltpu.roll(east_groups[r], 2, 0)
                else:
                    w, e = west_groups[3 * (r - 6) :], east_groups[3 * (r - 6) :]
                    low = jnp.where(
                        slot < 2, pltpu.roll(w[0], 2, 0), jnp.where(slot < 4, pltpu.roll(w[1], 4, 0), pltpu.roll(w[2], 6, 0))
                    )
                    high = jnp.where(
                        slot < 4, pltpu.roll(e[0], 4, 0), jnp.where(slot < 6, pltpu.roll(e[1], 6, 0), e[2])
                    )
                at = 16 * r
                rows.append(centre[g, a, at : at + 8] + jnp.where(slot < 6, low, 0.0))
                rows.append(centre[g, a, at + 8 : at + 16] + jnp.where(slot >= 2, high, 0.0))
            ref[:, lanes(g)] = jnp.concatenate(rows, axis=0).astype(jnp.bfloat16)

    wait_pair(own_copies())
    forward_strips(0)
    forward_strips(1)
    forward_strips(2)
    forward_strips(3)
    attend(0)
    attend(1)
    attend(2)
    return_sides(0)
    attend(3)
    return_sides(1)
    return_sides(2)
    return_sides(3)
    start_pair(back_own_copies())
    for g in range(CHUNKS):
        outputs(g)

    wait_pair(back_own_copies())

    @pl.when(has_south)
    def _():
        for g in range(CHUNKS):
            for a in range(2):
                centre[g, a, 32:128] += strips_in[0, g, a, 0:OWN].astype(jnp.float32)

    @pl.when(has_north)
    def _():
        for g in range(CHUNKS):
            for a in range(2):
                centre[g, a, 0:96] += strips_in[1, g, a, 0:OWN].astype(jnp.float32)

    for g in range(CHUNKS):
        finish(g)

    def wait_sent(copies):
        up, down = copies

        @pl.when(has_north)
        def _():
            up.wait_send()

        @pl.when(has_south)
        def _():
            down.wait_send()

    wait_sent(own_copies())
    wait_sent(back_own_copies())
    for g in range(CHUNKS):
        for copy in lon_copies(g) + back_lon_copies(g):
            copy.wait_send()
        wait_sent(lat_copies(g))
        wait_sent(back_lat_copies(g))


def write(*refs):
    sources, targets, sems = refs[:4], refs[4:8], refs[8]
    half = sources[0].shape[0] // 2
    copies = [
        pltpu.make_async_copy(s.at[pl.ds(half * j, half)], t.at[pl.ds(half * j, half)], sems.at[i, j])
        for i, (s, t) in enumerate(zip(sources, targets))
        for j in range(2)
    ]
    for copy in copies:
        copy.start()
    for copy in copies:
        copy.wait()


def shards(queries, key_cells, value_cells, grad_output, rel_bias):
    height, breadth, channels = queries.shape
    count = height * breadth
    flat = [x.reshape(count, channels) for x in (queries, key_cells, value_cells, grad_output)]
    bf16, f32 = jnp.bfloat16, jnp.float32
    hbm = pl.BlockSpec(memory_space=pltpu.HBM)
    shapes = [jax.ShapeDtypeStruct((count, channels), bf16)] * 4
    found = pl.pallas_call(
        kernel,
        out_shape=shapes,
        in_specs=[hbm] * 5,
        out_specs=[pl.BlockSpec(memory_space=pltpu.VMEM)] * 4,
        scratch_shapes=[pltpu.VMEM((count, channels), bf16)] * 4
        + [
            pltpu.VMEM(rel_bias.shape, f32),
            pltpu.VMEM((CHUNKS, 2, KEYS, 128), bf16),
            pltpu.VMEM((CHUNKS, 2, 2, SIDE, 128), bf16),
            pltpu.VMEM((CHUNKS, KEYS, 256), f32),
            pltpu.VMEM((24, 8, 128), f32),
            pltpu.VMEM((8, 512), f32),
            pltpu.VMEM((2, CHUNKS, 2, STRIP, 128), bf16),
            pltpu.VMEM((2, CHUNKS, 2, STRIP, 128), bf16),
            pltpu.VMEM((CHUNKS, 2, CENTRE, 128), f32),
            pltpu.VMEM((CHUNKS, 2, 2, SIDE, 128), bf16),
            pltpu.VMEM((CHUNKS, 2, 2, SIDE, 128), bf16),
            pltpu.VMEM((CHUNKS, 2, KEYS, 256), bf16),
        ]
        + [pltpu.SemaphoreType.DMA((CHUNKS, 2))] * 8
        + [pltpu.SemaphoreType.DMA((2, 2))] * 2
        + [pltpu.SemaphoreType.DMA((5,))],
        compiler_params=pltpu.CompilerParams(
            collective_id=0, has_side_effects=True, vmem_limit_bytes=LIMIT
        ),
        name="neighbourhood",
    )(*[pltpu.with_memory_space_constraint(x, pltpu.HBM) for x in flat + [rel_bias]])
    found = pl.pallas_call(
        write,
        out_shape=shapes,
        in_specs=[hbm] * 4,
        out_specs=[hbm] * 4,
        scratch_shapes=[pltpu.SemaphoreType.DMA((4, 2))],
        compiler_params=pltpu.CompilerParams(vmem_limit_bytes=LIMIT),
        name="write",
    )(*found)
    return tuple(x.reshape(height, breadth, channels) for x in found)


def solution(mesh):
    tiled = P("lat", "lon", None)
    return jax.shard_map(
        shards, mesh=mesh, in_specs=(tiled,) * 4 + (P(),), out_specs=(tiled,) * 4, check_vma=False
    )
```
